256 devices in a mesh: grp: 8 (over y, core), sub: 32 (over x, z).
Axes of the slice: x: 4, y: 4, z: 8, core: 2. Of those that a mesh axis runs over, the one named last changes fastest.
Arguments:
- right_side: float32 [65536, 2048], P(('grp', 'sub'))
- schur: bfloat16 [131072, 512], P(('grp', 'sub'))
- inv_factor: bfloat16 [131072, 512], P(('grp', 'sub'))
- coarse_inverse: float32 [2048, 256], P('grp')
- primal_index: int32 [256, 8], P(('grp', 'sub')), may hold values from 0 to 255
- phase: int32 [65536], P(('grp', 'sub')), may hold values from 0 to 3
- phase_coef: float32 [4], replicated, may hold values from 0.5 to 4
Outputs:
- solution: float32 [65536, 2048], P(('grp', 'sub'))
- residual: float32 [65536, 2048], P(('grp', 'sub'))
The draws below stay inside these ranges and needn't reach their ends.
All inputs are finite; a program needn't handle non-finite values.
Results may differ from the reference program's by a relative error of at most 0.0056.
Values may be sent and summed in bfloat16 or wider, within the bound.
A program may use at most 64 MiB of HBM per device.

```python
import math
import jax
import jax.numpy as jnp
from jax import lax

NI = 512
NF = 256
NPD = 8
NC = 256
NRHS = 2048
PHASES = 4
SUBS = 256
ROWS = 65536
N_GRP = 8
N_SUB = 32


def draw_right_side(key, part):
    k1, k2, k3 = jax.random.split(key, 3)
    place = jnp.arange(ROWS, dtype=jnp.float32) / ROWS
    row_scale = (0.5 + place) * jnp.exp(jax.random.uniform(k1, (ROWS,), jnp.float32, -1.15, 1.15))
    col_scale = jnp.exp(jax.random.uniform(k2, (NRHS,), jnp.float32, -1.15, 1.15))
    base = jax.random.normal(k3, (ROWS, NRHS), jnp.float32)
    return (row_scale[:, None] * col_scale[None, :] * base).astype(jnp.float32)


def square_eye(width):
    return (jnp.arange(width)[:, None] == jnp.arange(width)[None, :]).astype(jnp.float32)


def draw_schur(key, part):
    k1, k2 = jax.random.split(jax.random.fold_in(key, 11))
    noise = jax.random.normal(k1, (SUBS, NI, NI), jnp.float32)
    sym = 0.6 * (noise + jnp.swapaxes(noise, 1, 2)) / jnp.sqrt(2.0 * NI)
    diag = jax.random.uniform(k2, (SUBS, NI, 1), jnp.float32, 1.5, 3.5)
    return (sym + diag * square_eye(NI)[None]).reshape(SUBS * NI, NI).astype(jnp.bfloat16)


def draw_inv_factor(key, part):
    k1, k2 = jax.random.split(jax.random.fold_in(key, 23))
    noise = 0.5 * jax.random.normal(k1, (SUBS, NI, NI), jnp.float32) / jnp.sqrt(1.0 * NI)
    diag = jax.random.uniform(k2, (SUBS, NI, 1), jnp.float32, 0.8, 1.6)
    return (noise + diag * square_eye(NI)[None]).reshape(SUBS * NI, NI).astype(jnp.bfloat16)


def draw_coarse_inverse(key, part):
    k1, k2, k3 = jax.random.split(jax.random.fold_in(key, 37), 3)
    noise = 0.5 * jax.random.normal(k1, (N_GRP, NC, NC), jnp.float32) / jnp.sqrt(1.0 * NC)
    diag = jax.random.uniform(k2, (N_GRP, NC, 1), jnp.float32, 0.5, 1.0)
    order = jax.random.permutation(k3, N_GRP).astype(jnp.float32)
    level = order / max(N_GRP - 1, 1)
    group_scale = jnp.exp(level * jnp.log(16.0))
    matrix = (noise + diag * square_eye(NC)[None]) * group_scale[:, None, None]
    return matrix.reshape(N_GRP * NC, NC).astype(jnp.float32)


def place_ends(drawn, rng, smallest, high):
    index_at = [jax.random.randint(jax.random.fold_in(rng, axis), (), 0, length) for axis, length in enumerate(drawn.shape)]
    main_axis = drawn.shape.index(max(drawn.shape))
    neighbour = index_at[:main_axis] + [(index_at[main_axis] + 1) % drawn.shape[main_axis]] + index_at[main_axis + 1:]
    return drawn.at[tuple(index_at)].set(smallest).at[tuple(neighbour)].set(high)


def setup_inputs(seed: int = 0) -> dict:
    key_of = jax.random.split(jax.random.key(seed), 8)
    return {
        "right_side": draw_right_side(jax.random.fold_in(key_of[7], 71), 0),
        "schur": draw_schur(jax.random.fold_in(key_of[7], 71), 0),
        "inv_factor": draw_inv_factor(jax.random.fold_in(key_of[7], 71), 0),
        "coarse_inverse": draw_coarse_inverse(jax.random.fold_in(key_of[7], 71), 0),
        "primal_index": place_ends(jax.random.randint(key_of[4], (SUBS, NPD), 0, NF), jax.random.fold_in(key_of[4], 1), 0, NF - 1).astype(jnp.int32),
        "phase": place_ends(jax.random.randint(key_of[5], (ROWS,), 0, PHASES), jax.random.fold_in(key_of[5], 1), 0, PHASES - 1).astype(jnp.int32),
        "phase_coef": jnp.clip(jnp.exp(jax.random.uniform(key_of[6], (PHASES,), jnp.float32, math.log(0.5), math.log(4.0))), 0.5, 4.0),
    }


def extend(block):
    return jnp.concatenate([jnp.roll(block, 1, axis=0), block], axis=1)


def assemble(local):
    return local[:, NF:, :] + jnp.roll(local[:, :NF, :], -1, axis=0)


def reference(right_side, schur, inv_factor, coarse_inverse, primal_index, phase, phase_coef):
    hi = lax.Precision.HIGHEST
    rhs = right_side.reshape(N_GRP, N_SUB, NF, NRHS)
    panels = schur.reshape(N_GRP, N_SUB, NI, NI)
    factors = inv_factor.reshape(N_GRP, N_SUB, NI, NI)
    coarse = coarse_inverse.reshape(N_GRP, NC, NC)
    picks = primal_index.reshape(N_GRP, N_SUB, NPD)
    labels = phase.reshape(N_GRP, N_SUB, NF)
    onehot = (picks[..., None] == jnp.arange(NF, dtype=jnp.int32)).astype(jnp.float32)
    coarse_rhs = jnp.einsum('gskf,gsfr->gskr', onehot, rhs, precision=hi).reshape(N_GRP, NC, NRHS)
    solved = jnp.einsum('gab,gbr->gar', coarse, coarse_rhs, precision=hi)
    shared = jnp.sum(solved, axis=0) / N_GRP
    correction = (solved + shared[None]).reshape(N_GRP, N_SUB, NPD, NRHS)
    table = (jnp.arange(PHASES, dtype=jnp.int32)[None, None, :] == labels[..., None]).astype(jnp.float32)
    coef_rows = jnp.einsum('gsfk,k->gsf', table, phase_coef, precision=hi)

    def one_group(items):
        rhs_g, panel_g, factor_g, onehot_g, corr_g, coef_g = items
        rb = rhs_g.astype(jnp.bfloat16)
        fac = factor_g.astype(jnp.float32)
        first = jnp.einsum('sij,sjr->sir', fac, extend(rb).astype(jnp.float32)).astype(jnp.bfloat16)
        second = jnp.einsum('sji,sjr->sir', fac, first.astype(jnp.float32)).astype(jnp.bfloat16)
        direction = 0.5 * assemble(second.astype(jnp.float32)) + jnp.einsum('skf,skr->sfr', onehot_g, corr_g, precision=hi)
        dirb = direction.astype(jnp.bfloat16)
        rz_group = jnp.sum(rhs_g * direction, axis=(0, 1))
        image = jnp.einsum('sij,sjr->sir', panel_g.astype(jnp.float32), extend(dirb).astype(jnp.float32)).astype(jnp.bfloat16)
        qvec = assemble(image.astype(jnp.float32)) + coef_g[..., None] * dirb.astype(jnp.float32)
        return dirb, qvec, rz_group

    dirb, qvec, rz_parts = lax.map(one_group, (rhs, panels, factors, onehot, correction, coef_rows))
    rz_total = jnp.sum(rz_parts, axis=0)
    pq_total = jnp.sum(dirb.astype(jnp.float32) * qvec, axis=(0, 1, 2))
    alpha = rz_total / pq_total
    solution = (alpha * dirb.astype(jnp.float32)).reshape(ROWS, NRHS)
    residual = (rhs - alpha * qvec).reshape(ROWS, NRHS)
    return solution, residual
```

```python
import jax
import jax.numpy as jnp
from jax import lax
from jax.experimental import pallas as pl
from jax.experimental.pallas import tpu as pltpu
from jax.sharding import PartitionSpec as P

MESH = pl.DeviceIdType.MESH
F32 = jnp.float32
BF16 = jnp.bfloat16
NX, NZ = 4, 8
WIDTH = 256
AHEAD = 2
LAG = 2


def kernel(
    idx_ref, coef_ref, phase_ref, rs_hbm, g_hbm, s_hbm, k_hbm,
    zb_out, q_out, alpha_out,
    rs, gm, gt, sm, km, xs, vs, vl, vr, zs, ys, yl, yr, onehot, coef_col, esplit,
    rc, xg, rr, hb, hr, ag, eb, e5, e6, ara, arb, arc,
    load_sem, mat_sem, shift_send, shift_recv, co_send, co_recv, ar_send, ar_recv,
):
    n_grp, n_sub = lax.axis_size("grp"), lax.axis_size("sub")
    g, s = lax.axis_index("grp"), lax.axis_index("sub")
    x, z = lax.div(s, NZ), lax.rem(s, NZ)
    half, block = lax.div(z, 4), lax.rem(z, 4)
    right, left = lax.rem(s + 1, n_sub), lax.rem(s + n_sub - 1, n_sub)
    rows = rs.shape[1]
    chunks, width = rs.shape[0], rs.shape[2]
    per = width // 128
    upper, lower = pl.ds(0, rows), pl.ds(rows, rows)

    def x_peer(d):
        p = lax.rem(x + d, NX)
        return p, {"sub": p * NZ + z}

    def z_peer(d):
        p = lax.rem(z + d, NZ)
        return p, {"sub": x * NZ + p}

    def g_peer(d):
        p = lax.rem(g + d, n_grp)
        return p, {"grp": p}

    def load(c):
        return pltpu.make_async_copy(
            rs_hbm.at[:, pl.ds(c * width, width)], rs.at[c], load_sem.at[c]
        )

    mats = [
        pltpu.make_async_copy(src, dst, mat_sem.at[i])
        for i, (src, dst) in enumerate([(g_hbm, gm), (k_hbm, km), (s_hbm, sm)])
    ]

    def signal(to):
        pl.semaphore_signal(
            pltpu.get_barrier_semaphore(), inc=1, device_id=to, device_id_type=MESH
        )

    def remote(src, dst, send, recv, to):
        return pltpu.make_async_remote_copy(
            src_ref=src, dst_ref=dst, send_sem=send, recv_sem=recv,
            device_id=to, device_id_type=MESH,
        )

    def shift(which, c):
        src, dst, to = (
            (xs.at[c, lower], xs.at[c, upper], right),
            (vs.at[c], vr.at[c], left),
            (zs.at[c, lower], zs.at[c, upper], right),
            (ys.at[c], yr.at[c], left),
        )[which]
        return remote(src, dst, shift_send.at[which, c], shift_recv.at[which, c], {"sub": to})

    for peer, count in ((x_peer, NX), (z_peer, NZ), (g_peer, n_grp)):
        for d in range(1, count):
            signal(peer(d)[1])
    signal({"sub": right})
    signal({"sub": left})
    for c in range(chunks):
        load(c).start()
    for m in mats:
        m.start()

    lane = lax.broadcasted_iota(jnp.int32, onehot.shape, 1)
    row = lax.broadcasted_iota(jnp.int32, onehot.shape, 0)
    want = jnp.full(onehot.shape, -1, jnp.int32)
    for k in range(8):
        want = jnp.where((lax.rem(lane, 8) == k) & (lane < 24), idx_ref[0, k], want)
    onehot[...] = (want == row).astype(F32).astype(BF16)
    coef_row = jnp.zeros(phase_ref.shape, F32)
    for p in range(4):
        coef_row = jnp.where(phase_ref[...] == p, coef_ref[p], coef_row)
    coef_col[...] = jnp.transpose(jnp.broadcast_to(coef_row, (128, rows)))

    for c in range(chunks):
        load(c).wait()
        xs[c, lower] = rs[c].astype(BF16)

    pl.semaphore_wait(
        pltpu.get_barrier_semaphore(), NX - 1 + NZ - 1 + n_grp - 1 + 2
    )

    for c in range(AHEAD):
        shift(0, c).start()

    lane8 = lax.broadcasted_iota(jnp.int32, (8, rows), 1)
    row8 = lax.broadcasted_iota(jnp.int32, (8, rows), 0)
    want8 = jnp.full((8, rows), -1, jnp.int32)
    for k in range(8):
        want8 = jnp.where(row8 == k, idx_ref[0, k], want8)
    pick = (want8 == lane8).astype(F32)
    for c in range(chunks):
        picked = jnp.dot(
            pick, rs[c], precision=lax.Precision.HIGHEST, preferred_element_type=F32
        )
        for i in range(per):
            cb = c * per + i
            rc[cb // 4, cb % 4] = picked[:, i * 128 : (i + 1) * 128]

    def exchange(stage, peer, count, src, dst, me, send=co_send, recv=co_recv):
        def out(d):
            p, to = peer(d)
            return remote(src(p), dst(me), send.at[stage, p], recv.at[stage, me], to)

        def arriving(d):
            p, to = peer(d)
            return remote(src(p), dst(p), send.at[stage, p], recv.at[stage, p], to)

        def start():
            for d in range(1, count):
                out(d).start()

        def wait():
            for d in range(1, count):
                arriving(d).wait_recv()

        def drain():
            for d in range(1, count):
                out(d).wait_send()

        return start, wait, drain

    st1 = exchange(0, x_peer, NX, lambda p: rc.at[p], lambda me: xg.at[:, me], x)
    st2 = exchange(1, z_peer, NZ, lambda p: xg.at[lax.rem(p, 4)], lambda me: rr.at[:, me], z)
    st3 = exchange(2, g_peer, n_grp, lambda p: hb.at[p], lambda me: hr.at[me], g)
    st4 = exchange(3, g_peer, n_grp, lambda p: ag.at[g], lambda me: ag.at[me], g)
    st5 = exchange(
        4, z_peer, NZ, lambda p: eb.at[:, p],
        lambda me: e5.at[pl.ds(lax.div(me, 4) * 2, 2), lax.rem(me, 4)], z,
    )
    st6 = exchange(5, x_peer, NX, lambda p: e5.at[p], lambda me: e6.at[pl.ds(me * 4, 4)], x)

    xg[:, x] = rc[x]
    st1[0]()

    mats[0].wait()
    gt[...] = jnp.transpose(gm[...])
    mats[1].wait()
    mats[2].wait()

    def to_owners():
        st1[1]()
        rr[:, z] = xg[block]
        st2[0]()

    def solve():
        st2[1]()
        mine = km[pl.ds(pl.multiple_of(half * 128, 128), 128), :]
        solved = jnp.dot(
            mine, rr[...].reshape(256, 128),
            precision=lax.Precision.HIGHEST, preferred_element_type=F32,
        )
        hb[...] = solved.reshape(hb.shape)
        hr[g] = hb[g]
        st3[0]()

    def mean():
        st3[1]()
        total = hr[0]
        for p in range(1, n_grp):
            total = total + hr[p]
        ag[g] = total / n_grp
        st4[0]()

    def back():
        st4[1]()
        eb[...] = (hb[...] + ag[...]).reshape(eb.shape)
        e5[pl.ds(half * 2, 2), block] = eb[:, z]
        st5[0]()

    def spread():
        st5[1]()
        e6[pl.ds(x * 4, 4)] = e5[x]
        st6[0]()

    events = {0: to_owners, 3: solve, 4: mean, 5: back, 7: spread}

    def first(c, _):
        shift(0, c).wait_recv()

        @pl.when(c + AHEAD < chunks)
        def _():
            shift(0, c + AHEAD).start()

        u = jnp.dot(gm[...], xs[c], preferred_element_type=F32).astype(BF16)
        v = jnp.dot(gt[...], u, preferred_element_type=F32).astype(BF16)
        vs[c] = v[:rows]
        shift(1, c).start()
        vl[c] = v[rows:]
        for at, event in events.items():
            pl.when(c == at)(event)
        return 0

    lax.fori_loop(0, chunks, first, 0)

    st6[1]()
    for cb in range(NX * 4):
        c, off = cb // per, (cb % per) * 128
        e = e6[cb]
        e1 = e.astype(BF16)
        rest = e - e1.astype(F32)
        e2 = rest.astype(BF16)
        e3 = (rest - e2.astype(F32)).astype(BF16)
        parts = [e1.astype(F32), e2.astype(F32), e3.astype(F32), jnp.zeros_like(e)]
        esplit[c, :, pl.ds(off, 128)] = jnp.concatenate(parts, axis=0).astype(BF16)

    coef = jnp.concatenate([coef_col[...]] * per, axis=1)

    def second(c):
        shift(1, c).wait_recv()
        scattered = jnp.dot(onehot[...], esplit[c], preferred_element_type=F32)
        direction = 0.5 * (vl[c].astype(F32) + vr[c].astype(F32)) + scattered
        zs[c, lower] = direction.astype(BF16)
        shift(2, c).start()
        ara[g, c, 0:1] = jnp.sum(rs[c] * direction, axis=0, keepdims=True)

    def third(c):
        shift(2, c).wait_recv()
        y = jnp.dot(sm[...], zs[c], preferred_element_type=F32).astype(BF16)
        ys[c] = y[:rows]
        shift(3, c).start()
        yl[c] = y[rows:]
        both = zs[c].astype(F32) * y.astype(F32)
        own = zs[c, lower].astype(F32)
        terms = both[:rows] + both[rows:] + coef * own * own
        ara[g, c, 1:2] = jnp.sum(terms, axis=0, keepdims=True)

    def fourth(c):
        shift(3, c).wait_recv()
        own = zs[c, lower]
        cols = pl.ds(pl.multiple_of(c * width, width), width)
        zb_out[:, cols] = own
        q_out[:, cols] = yl[c].astype(F32) + yr[c].astype(F32) + coef * own.astype(F32)

    for c in range(AHEAD):
        second(c)

    def rest(c, _):
        @pl.when(c + AHEAD < chunks)
        def _():
            second(c + AHEAD)

        third(c)

        @pl.when(c >= LAG)
        def _():
            fourth(c - LAG)

        return 0

    lax.fori_loop(0, chunks, rest, 0)

    sta = exchange(0, g_peer, n_grp, lambda p: ara.at[g], lambda me: ara.at[me], g, ar_send, ar_recv)
    stb = exchange(1, x_peer, NX, lambda p: arb.at[x], lambda me: arb.at[me], x, ar_send, ar_recv)
    stc = exchange(2, z_peer, NZ, lambda p: arc.at[z], lambda me: arc.at[me], z, ar_send, ar_recv)

    def total(buf, count):
        acc = buf[0]
        for p in range(1, count):
            acc = acc + buf[p]
        return acc

    sta[0]()
    for c in range(chunks - LAG, chunks - LAG + 1):
        fourth(c)
    sta[1]()
    arb[x] = total(ara, n_grp)
    stb[0]()
    for c in range(chunks - LAG + 1, chunks):
        fourth(c)
    stb[1]()
    arc[z] = total(arb, NX)
    stc[0]()
    stc[1]()
    sums = total(arc, NZ)
    for c in range(chunks):
        alpha_out[:, pl.ds(c * width, width)] = sums[c, 0:1] / sums[c, 1:2]

    for st in (st1, st2, st3, st4, st5, st6, sta, stb, stc):
        st[2]()

    def drain(c, _):
        for which in range(4):
            shift(which, c).wait_send()
        return 0

    lax.fori_loop(0, chunks, drain, 0)


def body(right_side, schur, inv_factor, coarse_inverse, primal_index, phase, phase_coef):
    rows, cols = right_side.shape
    n = cols // WIDTH
    n_grp = lax.axis_size("grp")
    smem = pl.BlockSpec(memory_space=pltpu.SMEM)
    vmem = pl.BlockSpec(memory_space=pltpu.VMEM)
    hbm = pl.BlockSpec(memory_space=pl.ANY)
    chunked = pltpu.VMEM((n, rows, WIDTH), BF16)
    stacked = pltpu.VMEM((n, 2 * rows, WIDTH), BF16)
    square = pltpu.VMEM(schur.shape, BF16)
    dma = pltpu.SemaphoreType.DMA
    zb, q, alpha = pl.pallas_call(
        kernel,
        out_shape=(
            jax.ShapeDtypeStruct((rows, cols), BF16),
            jax.ShapeDtypeStruct((rows, cols), F32),
            jax.ShapeDtypeStruct((1, cols), F32),
        ),
        in_specs=[smem, smem, vmem, hbm, hbm, hbm, hbm],
        out_specs=(vmem, vmem, vmem),
        scratch_shapes=[
            pltpu.VMEM((n, rows, WIDTH), F32),
            square, square, square,
            pltpu.VMEM(coarse_inverse.shape, F32),
            stacked, chunked, chunked, chunked, stacked, chunked, chunked, chunked,
            pltpu.VMEM((rows, 32), BF16),
            pltpu.VMEM((rows, 128), F32),
            pltpu.VMEM((n, 32, WIDTH), BF16),
            pltpu.VMEM((NX, 4, 8, 128), F32),
            pltpu.VMEM((4, NX, 8, 128), F32),
            pltpu.VMEM((NX, NZ, 8, 128), F32),
            pltpu.VMEM((n_grp, 16, 128), F32),
            pltpu.VMEM((n_grp, 16, 128), F32),
            pltpu.VMEM((n_grp, 16, 128), F32),
            pltpu.VMEM((2, NZ, 8, 128), F32),
            pltpu.VMEM((NX, 4, 8, 128), F32),
            pltpu.VMEM((NX * 4, 8, 128), F32),
            pltpu.VMEM((n_grp, n, 2, WIDTH), F32),
            pltpu.VMEM((NX, n, 2, WIDTH), F32),
            pltpu.VMEM((NZ, n, 2, WIDTH), F32),
            dma((n,)), dma((3,)), dma((4, n)), dma((4, n)),
            dma((6, 8)), dma((6, 8)), dma((3, 8)), dma((3, 8)),
        ],
        compiler_params=pltpu.CompilerParams(
            collective_id=0, has_side_effects=True, vmem_limit_bytes=56 * 2**20
        ),
    )(
        primal_index, phase_coef, phase.reshape(1, rows),
        right_side, inv_factor, schur, coarse_inverse,
    )
    return alpha * zb.astype(F32), right_side - alpha * q


def solution(mesh):
    in_specs = (
        P(("grp", "sub"), None),
        P(("grp", "sub"), None),
        P(("grp", "sub"), None),
        P("grp", None),
        P(("grp", "sub"), None),
        P(("grp", "sub")),
        P(),
    )
    out_specs = (P(("grp", "sub"), None), P(("grp", "sub"), None))
    return jax.shard_map(body, mesh=mesh, in_specs=in_specs, out_specs=out_specs, check_vma=False)
```
